32 devices in a mesh: seq: 16 (over z, y, x), span: 2 (over core).
Axes of the slice: x: 2, y: 2, z: 4, core: 2. Of those that a mesh axis runs over, the one named last changes fastest.
Arguments:
- query: bfloat16 [2, 2048, 3072], P('span', 'seq'), may hold values from -180 to 180
- dout: bfloat16 [2, 2048, 3072], P('span', 'seq'), may hold values from -16 to 16
- mem_key: bfloat16 [2, 768, 3072], P('span', 'seq'), may hold values from -7 to 7
- mem_value: bfloat16 [2, 768, 3072], P('span', 'seq'), may hold values from -6 to 6
- keep_count: int32 [2, 16], P('span'), may hold values from 1 to 48, 256 in all within a row
- keep_slot: int32 [2, 768, 4], P('span', 'seq'), may hold values from 0 to 127
- pool_weight: float32 [2, 768, 4], P('span', 'seq'), may hold values from 0.5 to 1.5
Outputs:
- dquery: bfloat16 [2, 2048, 3072], P('span', 'seq')
- dkey_tok: bfloat16 [2, 2048, 3072], P('span', 'seq')
- dvalue_tok: bfloat16 [2, 2048, 3072], P('span', 'seq')
The draws below stay inside these ranges and needn't reach their ends.
Inputs may be any that keep to these rules, and one draw needn't show every extreme that they name: `keep_count`: each span's counts sum to 256, and the largest is 48.
All inputs are finite; a program needn't handle non-finite values.
Results may differ from the reference program's by a relative error of at most 0.011.
Values may be sent and summed in bfloat16 or wider, within the bound.
A program may use at most 64 MiB of HBM per device.

```python
import math
import jax
import jax.numpy as jnp
import numpy as np
from jax import lax

HEADS = 24
HEAD_DIM = 128
POOL = 4
TOK_DEV = 128
MEM = 256
WIDTH = 3072
TOKENS = 2048
SPANS = 2
OWNERS = 16
CAP = 48
SLOTS = 768


def joint_draw(key):
    key_query, key_memory = jax.random.split(jax.random.fold_in(key, 11), 2)
    query_raw = jnp.clip(jax.random.normal(key_query, (SPANS, TOKENS, WIDTH), jnp.float32), -6.0, 6.0)
    memory_raw = jnp.clip(jax.random.normal(key_memory, (SPANS, SLOTS, WIDTH), jnp.float32), -6.0, 6.0)
    return (query_raw, memory_raw)


def draw_query(key, part):
    return joint_draw(key)[0].astype(jnp.bfloat16)


def draw_mem_key(key, part):
    return joint_draw(key)[1].astype(jnp.bfloat16)


def with_ends(entries, rng, smallest, top_value):
    longest = entries.shape.index(max(entries.shape))
    spots = []
    for shift in (0, 1):
        where = [jax.random.randint(jax.random.fold_in(rng, axis), (), 0, length) for axis, length in enumerate(entries.shape)]
        where[longest] = (where[longest] + shift) % entries.shape[longest]
        spots.append(tuple(where))
    return entries.at[spots[0]].set(smallest).at[spots[1]].set(top_value)


def level_of(key, dims, cuts, smallest, high):
    loudness = 1.0
    for position, shards_of in cuts:
        draws = jax.random.uniform(jax.random.fold_in(jax.random.fold_in(key, 6), position), (shards_of,), jnp.float32, smallest / len(cuts), high / len(cuts))
        loudness = loudness * jnp.repeat(jnp.exp(draws), dims[position] // shards_of).reshape((-1,) + (1,) * (len(dims) - 1 - position))
    return loudness


def profile(number_of, total, bound, slope):
    loads = [(1 << 20) // math.isqrt(standing ** slope) + 1 for standing in range(2, number_of + 1)]
    surplus, counts = total - bound - (number_of - 1), [1] * (number_of - 1)
    while surplus > 0:
        movable = [i for i in range(number_of - 1) if counts[i] < bound]
        pool, remaining = sum([loads[i] for i in movable]), surplus
        for i in movable:
            more = min(bound - counts[i], max(1, remaining * loads[i] // pool), surplus)
            counts[i] = counts[i] + more
            surplus = surplus - more
    return np.array([bound] + counts)


def ragged_sizes(stream_key, count, total, limit, skew):
    if count == 2:
        one = jax.random.randint(stream_key, (), max(1, total - limit), min(limit, total - 1) + 1)
        return jnp.stack([one, total - one])
    sizes = jnp.asarray(profile(count, total, limit, skew), jnp.int32)
    pairs = (count - 1) // 2
    donor, receiver = sizes[1:1 + 2 * pairs:2], sizes[2:2 + 2 * pairs:2]
    margin = jnp.minimum(donor - 1, limit - receiver)
    moved = jax.random.randint(jax.random.fold_in(stream_key, 1), (pairs,), 0, 1 << 20) % (margin + 1)
    sizes = sizes.at[1:1 + 2 * pairs:2].set(donor - moved).at[2:2 + 2 * pairs:2].set(receiver + moved)
    return sizes[jax.random.permutation(jax.random.fold_in(stream_key, 2), count)]


def scatter_about(rng, shape, width, bound, shards=(), kind=jnp.bfloat16):
    loudness = level_of(rng, shape, shards, -0.22, 0.18) if shards else 1.0
    entries = jax.random.normal(rng, shape, jnp.float32) * width * loudness
    return jnp.minimum(jnp.maximum(entries, -bound), bound).astype(kind)


def setup_inputs(seed: int = 0) -> dict:
    arg_keys = jax.random.split(jax.random.key(seed), 8)
    query = draw_query(jax.random.fold_in(arg_keys[7], 71), 0)
    dout = scatter_about(arg_keys[1], (SPANS, TOKENS, WIDTH), 4.0, 16.0, ((0, 2), (1, 16)))
    mem_key = draw_mem_key(jax.random.fold_in(arg_keys[7], 71), 0)
    mem_value = scatter_about(arg_keys[3], (SPANS, SLOTS, WIDTH), 1.0, 6.0, ((0, 2), (1, 16)))
    keep_count = jax.vmap(lambda own: ragged_sizes(own, OWNERS, MEM, CAP, 2))(jax.random.split(arg_keys[4], SPANS)).reshape((SPANS, OWNERS)).astype(jnp.int32)
    keep_slot = with_ends(jax.random.randint(arg_keys[5], (SPANS, SLOTS, POOL), 0, TOK_DEV), jax.random.fold_in(arg_keys[5], 1), 0, TOK_DEV - 1).astype(jnp.int32)
    pool_weight = jnp.clip(0.5 + 1.0 * jax.random.uniform(arg_keys[6], (SPANS, SLOTS, POOL), jnp.float32) ** level_of(arg_keys[6], (SPANS, SLOTS, POOL), ((0, 2), (1, 16)), -0.2, 0.2), 0.5, 1.5)
    return {"query": query, "dout": dout, "mem_key": mem_key, "mem_value": mem_value, "keep_count": keep_count, "keep_slot": keep_slot, "pool_weight": pool_weight}


def full_backward(query_head, grad_head, key_head, value_head, live_mask):
    score_scale = HEAD_DIM ** -0.5
    scores = jnp.dot(query_head, key_head.T, preferred_element_type=jnp.float32) * score_scale
    scores = jnp.where(live_mask[None, :], scores, -jnp.inf)
    shifted = jnp.exp(scores - jnp.max(scores, axis=1, keepdims=True))
    probs_full = shifted / jnp.sum(shifted, axis=1, keepdims=True)
    probs_low = probs_full.astype(jnp.bfloat16)
    attn_out = jnp.dot(probs_low, value_head, preferred_element_type=jnp.float32)
    deltas = jnp.sum(grad_head.astype(jnp.float32) * attn_out, axis=1, keepdims=True)
    probs_grad = jnp.dot(grad_head, value_head.T, preferred_element_type=jnp.float32)
    scores_grad = (probs_full * (probs_grad - deltas)).astype(jnp.bfloat16)
    query_grad = (jnp.dot(scores_grad, key_head, preferred_element_type=jnp.float32) * score_scale).astype(jnp.bfloat16)
    key_grad = jnp.dot(scores_grad.T, query_head, preferred_element_type=jnp.float32) * score_scale
    value_grad = jnp.dot(probs_low.T, grad_head, preferred_element_type=jnp.float32)
    return query_grad, key_grad, value_grad


def split_heads(values, length):
    return jnp.moveaxis(values.reshape(length, HEADS, HEAD_DIM), 1, 0)


def reference(query, dout, mem_key, mem_value, keep_count, keep_slot, pool_weight):
    query_grads = []
    pooled = []
    for span_index in range(SPANS):
        live_mask = (jnp.arange(SLOTS) % CAP) < jnp.repeat(keep_count[span_index], CAP)

        def one_head(pieces):
            return full_backward(pieces[0], pieces[1], pieces[2], pieces[3], live_mask)

        head_query, head_key, head_value = lax.map(one_head, (split_heads(query[span_index], TOKENS), split_heads(dout[span_index], TOKENS), split_heads(mem_key[span_index], SLOTS), split_heads(mem_value[span_index], SLOTS)))
        query_grads.append(jnp.moveaxis(head_query, 0, 1).reshape(TOKENS, WIDTH))
        key_grad = jnp.moveaxis(head_key, 0, 1).reshape(SLOTS, WIDTH)
        value_grad = jnp.moveaxis(head_value, 0, 1).reshape(SLOTS, WIDTH)
        positions = jnp.arange(TOK_DEV).astype(jnp.int32)
        onehot = (keep_slot[span_index].reshape(OWNERS, CAP, POOL)[..., None] == positions).astype(jnp.float32)
        matrix = jnp.einsum("scjt,scj->stc", onehot, pool_weight[span_index].reshape(OWNERS, CAP, POOL), precision=lax.Precision.HIGHEST)
        stacked = jnp.concatenate([key_grad, value_grad], axis=1).reshape(OWNERS, CAP, 2 * WIDTH)
        tokens_grad = jnp.einsum("stc,scw->stw", matrix, stacked, precision=lax.Precision.HIGHEST)
        pooled.append(tokens_grad.reshape(TOKENS, 2 * WIDTH))
    zero_rows = jnp.zeros((TOKENS, 2 * WIDTH), jnp.float32)
    handed = jnp.stack(pooled[1:] + [zero_rows]).astype(jnp.bfloat16)
    return jnp.stack(query_grads), handed[:, :, :WIDTH], handed[:, :, WIDTH:]
```

```python
import math

import jax
import jax.numpy as jnp
from jax import lax
from jax.experimental import pallas as pl
from jax.experimental.pallas import tpu as pltpu
from jax.sharding import PartitionSpec as P

HEAD_DIM = 128
LIVE = 256
HALF = LIVE // 2
BF = jnp.bfloat16
F32 = jnp.float32


def passed_along(block, axis, distance):
    devices = range(lax.axis_size(axis))
    route = [(i - distance, i) for i in devices if i - distance in devices]
    return lax.ppermute(block, axis, route)


def head_backward(query_head, grad_head, key_head, value_head, live_mask, block_rows):
    score_scale = key_head.shape[1] ** (-0.5)
    head_width = query_head.shape[1]
    blocks = query_head.shape[0] // block_rows
    query_blocks = query_head.reshape(blocks, block_rows, head_width)
    grad_blocks = grad_head.reshape(blocks, block_rows, head_width)

    def visit_block(totals, inputs):
        key_grad, value_grad = totals
        query_block, grad_block = inputs
        scores = jnp.dot(query_block, key_head.T, preferred_element_type=jnp.float32) * score_scale
        scores = jnp.where(live_mask[None, :], scores, -jnp.inf)
        shifted = jnp.exp(scores - jnp.max(scores, axis=1, keepdims=True))
        probs_full = shifted / jnp.sum(shifted, axis=1, keepdims=True)
        probs_low = probs_full.astype(jnp.bfloat16)
        attn_out = jnp.dot(probs_low, value_head, preferred_element_type=jnp.float32)
        deltas = jnp.sum(grad_block.astype(jnp.float32) * attn_out, axis=1, keepdims=True)
        probs_grad = jnp.dot(grad_block, value_head.T, preferred_element_type=jnp.float32)
        scores_grad = (probs_full * (probs_grad - deltas)).astype(jnp.bfloat16)
        query_grad = (
            jnp.dot(scores_grad, key_head, preferred_element_type=jnp.float32) * score_scale
        ).astype(jnp.bfloat16)
        key_grad = (
            key_grad
            + lax.dot_general(
                scores_grad,
                query_block,
                (((0,), (0,)), ((), ())),
                preferred_element_type=jnp.float32,
            )
            * score_scale
        )
        value_grad = value_grad + lax.dot_general(
            probs_low, grad_block, (((0,), (0,)), ((), ())), preferred_element_type=jnp.float32
        )
        return ((key_grad, value_grad), query_grad)

    empty_grad = jnp.zeros(key_head.shape, jnp.float32)
    (key_grad, value_grad), query_grad = lax.scan(
        visit_block, (empty_grad, empty_grad), (query_blocks, grad_blocks)
    )
    return (query_grad.reshape(-1, head_width), key_grad, value_grad)


def owner_rows(key_parts, value_parts, token_parts, groups, row_count):
    got_key, got_value = (
        lax.all_to_all(key_parts, "seq", split_axis=0, concat_axis=0, tiled=True),
        lax.all_to_all(value_parts, "seq", split_axis=0, concat_axis=0, tiled=True),
    )

    def fold_parts(values):
        shaped = values.reshape(token_parts, groups, row_count, values.shape[2], values.shape[3])
        summed = jnp.sum(shaped, axis=0)
        return summed.transpose(1, 0, 2, 3).reshape(row_count, -1)

    return (fold_parts(got_key), fold_parts(got_value))


def pool_matrix(slots, weights, local_tokens):
    positions = jnp.arange(local_tokens)
    onehot = (slots[:, :, None] == positions[None, None, :]).astype(jnp.float32)
    return jnp.einsum("cjt,cj->tc", onehot, weights, precision=lax.Precision.HIGHEST)


def apply_pool(matrix, key_rows, value_rows):
    stacked = jnp.concatenate([key_rows, value_rows], axis=1)
    return jnp.dot(
        matrix, stacked, precision=lax.Precision.HIGHEST, preferred_element_type=jnp.float32
    )


def per_device(query, dout, mem_key, mem_value, keep_count, keep_slot, pool_weight):
    devices = lax.axis_size("seq")
    head_width = HEAD_DIM
    head_count = query.shape[2] // head_width
    groups = math.gcd(head_count, devices)
    token_parts = devices // groups
    group_heads = head_count // groups
    local_tokens = query.shape[1]
    part_rows = local_tokens // token_parts
    capacity = mem_key.shape[1]
    owner_counts = keep_count[0]

    def token_layout(values):
        shaped = values.reshape(token_parts, part_rows, groups, group_heads, head_width)
        return shaped.transpose(0, 2, 1, 3, 4).reshape(devices, part_rows, group_heads, head_width)

    def memory_layout(values):
        row_count = values.shape[0]
        shaped = values.reshape(row_count, groups, group_heads, head_width).transpose(1, 0, 2, 3)
        spread = jnp.broadcast_to(shaped[None], (token_parts,) + shaped.shape)
        return spread.reshape(devices, row_count, group_heads, head_width)

    slot_index = jnp.arange(devices * capacity)
    live_mask = slot_index % capacity < jnp.repeat(owner_counts, capacity)
    key_used, value_used = (mem_key[0], mem_value[0])
    query_rows = lax.all_to_all(
        token_layout(query[0]), "seq", split_axis=0, concat_axis=0, tiled=True
    )
    grad_rows = lax.all_to_all(
        token_layout(dout[0]), "seq", split_axis=0, concat_axis=0, tiled=True
    )
    key_rows = lax.all_to_all(
        memory_layout(key_used), "seq", split_axis=0, concat_axis=0, tiled=True
    )
    value_rows = lax.all_to_all(
        memory_layout(value_used), "seq", split_axis=0, concat_axis=0, tiled=True
    )
    item_heads = query_rows.shape[2]
    row_count = key_rows.shape[1]
    query_total = devices * part_rows
    block_rows = 512
    query_flat = jnp.moveaxis(query_rows.reshape(query_total, item_heads, head_width), 1, 0)
    grad_flat = jnp.moveaxis(grad_rows.reshape(query_total, item_heads, head_width), 1, 0)
    key_flat = jnp.moveaxis(key_rows.reshape(devices * row_count, item_heads, head_width), 1, 0)
    value_flat = jnp.moveaxis(value_rows.reshape(devices * row_count, item_heads, head_width), 1, 0)

    def one_head(pieces):
        return head_backward(pieces[0], pieces[1], pieces[2], pieces[3], live_mask, block_rows)

    query_grad, key_grad, value_grad = lax.map(
        one_head, (query_flat, grad_flat, key_flat, value_flat)
    )
    query_back = jnp.moveaxis(query_grad, 0, 1).reshape(devices, part_rows, item_heads, head_width)
    key_back = jnp.moveaxis(key_grad, 0, 1).reshape(devices, row_count, item_heads, head_width)
    value_back = jnp.moveaxis(value_grad, 0, 1).reshape(devices, row_count, item_heads, head_width)
    returned = lax.all_to_all(query_back, "seq", split_axis=0, concat_axis=0, tiled=True)
    returned = returned.reshape(token_parts, groups, part_rows, group_heads, head_width).transpose(
        0, 2, 1, 3, 4
    )
    dquery = returned.reshape(1, local_tokens, groups * group_heads * head_width)
    matrix = pool_matrix(keep_slot[0], pool_weight[0], local_tokens)
    key_rows, value_rows = owner_rows(key_back, value_back, token_parts, groups, capacity)
    local_grad = apply_pool(matrix, key_rows, value_rows).astype(jnp.bfloat16)
    tokens_grad = passed_along(local_grad, "span", -1)
    feature_width = groups * group_heads * head_width
    dkey_tok = tokens_grad[None, :, :feature_width]
    dvalue_tok = tokens_grad[None, :, feature_width:]
    return (dquery, dkey_tok, dvalue_tok)


def copy_to(src, dst, send_sem, recv_sem, seq, span):
    return pltpu.make_async_remote_copy(
        src_ref=src,
        dst_ref=dst,
        send_sem=send_sem,
        recv_sem=recv_sem,
        device_id={"seq": seq, "span": span},
        device_id_type=pl.DeviceIdType.MESH,
    )


def fused_kernel(
    q_ref, g_ref, k_ref, v_ref, idx_ref, idxt_ref, slot_ref, weight_ref,
    dq_ref, dk_ref, dv_ref,
    kvin, rows, kv, acc, out16, ra, rb, r2a, r2b, r2send, r3, r3send, back_send, back,
    pool_send, pool_got,
    a_send, a_recv, z_send, xy_send, f_send, kv_recv,
    r1_send, ra_recv, rb_recv, r2_send, r2_recv, r3_send, r3_recv,
    b_send, b_recv, p_send, p_recv,
):
    n = 16
    me = lax.axis_index("seq")
    span = lax.axis_index("span")
    other = 1 - span
    capacity = k_ref.shape[0]
    cols = kv.shape[3]
    z, y, x = me // 4, (me // 2) % 2, me % 2
    xn = me + 1 - 2 * x
    yn = me + 2 - 4 * y
    own_line = me % 4
    x_line = xn % 4
    y_line = yn % 4
    d_line = 3 - own_line
    scale = HEAD_DIM ** (-0.5)

    barrier = pltpu.get_barrier_semaphore()
    for off in range(1, n):
        pl.semaphore_signal(
            barrier, inc=1, device_id={"seq": (me + off) % n, "span": span},
            device_id_type=pl.DeviceIdType.MESH,
        )
    for off in range(n):
        pl.semaphore_signal(
            barrier, inc=1, device_id={"seq": (me + off) % n, "span": other},
            device_id_type=pl.DeviceIdType.MESH,
        )
    for p in range(n // 2):
        kvin[p] = k_ref[:, p * cols : (p + 1) * cols]
        kvin[n // 2 + p] = v_ref[:, p * cols : (p + 1) * cols]
    pl.semaphore_wait(barrier, 2 * n - 1)

    def spread(off):
        p = (me + off) % n
        return copy_to(kvin.at[p], rows.at[me], a_send.at[off], a_recv.at[me], p, span)

    for off in range(1, n):
        spread(off).start()
    rows[me] = kvin[me]

    @pl.when(span == 1)
    def _():
        lanes = lax.broadcasted_iota(jnp.int32, pool_send.shape, 1)
        total = jnp.zeros(pool_send.shape, F32)
        for j in range(slot_ref.shape[1]):
            total = total + jnp.where(lanes == slot_ref[:, j : j + 1], weight_ref[:, j : j + 1], 0.0)
        pool_send[...] = total
        copy_to(pool_send, pool_got, p_send, p_recv, me, other).start()

    picks = lax.broadcasted_iota(jnp.int32, (LIVE, n * capacity), 0) == idx_ref[...]
    picks = jnp.where(picks, 1.0, 0.0).astype(BF)
    for off in range(1, n):
        p = (me + off) % n
        copy_to(kvin.at[p], rows.at[p], a_send.at[off], a_recv.at[p], p, span).wait_recv()
    packed = jnp.dot(picks, rows[...].reshape(n * capacity, cols), preferred_element_type=F32)
    kv[me] = packed.astype(BF).reshape(2, HALF, cols)

    def move(block, half, sem, target):
        return copy_to(kv.at[block, half], kv.at[block, half], sem, kv_recv.at[block, half], target, span)

    def arrived(block, half):
        move(block, half, z_send.at[0, 0], xn).wait_recv()

    def along_z(k):
        return ((z + k) % 4) * 4 + own_line

    for half in range(2):
        for k in (1, 3, 2):
            move(me, half, z_send.at[k, half], along_z(k)).start()
    for k in (0, 1, 3, 2):
        block = along_z(k)
        if k:
            arrived(block, 0)
            arrived(block, 1)
        move(block, 0, xy_send.at[k, 0, 0], xn).start()
        move(block, 1, xy_send.at[k, 1, 1], yn).start()
        move(block, 1, xy_send.at[k, 0, 1], xn).start()
        move(block, 0, xy_send.at[k, 1, 0], yn).start()

    def compute_line(line):
        def triple(zz, carry):
            t = zz * 4 + line
            start = pl.multiple_of(t * cols, 128)
            for h in range(cols // HEAD_DIM):
                here = pl.ds(pl.multiple_of(start + h * HEAD_DIM, 128), HEAD_DIM)
                inner = slice(h * HEAD_DIM, (h + 1) * HEAD_DIM)
                query = q_ref[:, here]
                grad = g_ref[:, here]
                key = kv[t, :, :, inner].reshape(LIVE, HEAD_DIM)
                value = kv[t + 8, :, :, inner].reshape(LIVE, HEAD_DIM)
                last = (((1,), (1,)), ((), ()))
                first = (((0,), (0,)), ((), ()))
                scores = lax.dot_general(query, key, last, preferred_element_type=F32) * scale
                shifted = jnp.exp(scores - jnp.max(scores, axis=1, keepdims=True))
                probs = shifted / jnp.sum(shifted, axis=1, keepdims=True)
                low = probs.astype(BF)
                probs_grad = lax.dot_general(grad, value, last, preferred_element_type=F32)
                delta = jnp.sum(low.astype(F32) * probs_grad, axis=1, keepdims=True)
                scores_grad = (probs * (probs_grad - delta)).astype(BF)
                dq = jnp.dot(scores_grad, key, preferred_element_type=F32) * scale
                dq_ref[:, here] = dq.astype(BF)

                @pl.when(span == 1)
                def _():
                    dkey = lax.dot_general(scores_grad, query, first, preferred_element_type=F32)
                    dkey = (dkey * scale).reshape(2, HALF, HEAD_DIM)
                    dvalue = lax.dot_general(low, grad, first, preferred_element_type=F32)
                    dvalue = dvalue.reshape(2, HALF, HEAD_DIM)
                    acc[t, :, :, inner] = dkey
                    acc[t + 8, :, :, inner] = dvalue
                    out16[t, :, :, inner] = dkey.astype(BF)
                    out16[t + 8, :, :, inner] = dvalue.astype(BF)

            return carry

        lax.fori_loop(0, 2, triple, 0)

    def send_a(line, slot, zz):
        return copy_to(
            out16.at[zz * 4 + line, 0], ra.at[slot, zz], r1_send.at[0, slot, zz], ra_recv.at[slot, zz], yn, span
        )

    def send_b(line, slot, zz):
        return copy_to(
            out16.at[zz * 4 + line, 1], rb.at[slot, zz], r1_send.at[1, slot, zz], rb_recv.at[slot, zz], xn, span
        )

    compute_line(own_line)
    for zz in (0, 1, 2, 3):
        bx, by = zz * 4 + x_line, zz * 4 + y_line
        arrived(bx, 0)
        move(bx, 0, f_send.at[zz, 0], yn).start()
        arrived(by, 1)
        move(by, 1, f_send.at[zz, 1], xn).start()
    for zz in range(4):
        arrived(zz * 4 + x_line, 1)
    compute_line(x_line)

    @pl.when(span == 1)
    def _():
        for zz in range(4):
            send_b(x_line, 0, zz).start()

    for zz in range(4):
        arrived(zz * 4 + y_line, 0)
    compute_line(y_line)

    @pl.when(span == 1)
    def _():
        for zz in range(4):
            send_a(y_line, 0, zz).start()

    for zz in range(4):
        for half in range(2):
            arrived(zz * 4 + d_line, half)
    compute_line(d_line)

    def second(zz, side):
        if side == 0:
            return copy_to(r2send.at[zz, 0], r2a.at[zz], r2_send.at[zz, 0], r2_recv.at[zz, 0], xn, span)
        return copy_to(r2send.at[zz, 1], r2b.at[zz], r2_send.at[zz, 1], r2_recv.at[zz, 1], yn, span)

    def third(k):
        return copy_to(r3send.at[k], r3.at[k], r3_send.at[k], r3_recv.at[k], along_z(k), span)

    def give(off):
        p = (me + off) % n
        return copy_to(back_send.at[p], back.at[me], b_send.at[off], b_recv.at[me], p, other)

    @pl.when(span == 1)
    def _():
        for zz in range(4):
            send_a(d_line, 1, zz).start()
            send_b(d_line, 1, zz).start()
        for zz in range(4):
            send_a(d_line, 1, zz).wait_recv()
            r2send[zz, 0] = (acc[zz * 4 + x_line, 0] + ra[1, zz].astype(F32)).astype(BF)
            second(zz, 0).start()
            send_b(d_line, 1, zz).wait_recv()
            r2send[zz, 1] = (acc[zz * 4 + y_line, 1] + rb[1, zz].astype(F32)).astype(BF)
            second(zz, 1).start()
        for zz in range(4):
            send_a(y_line, 0, zz).wait_recv()
            send_b(x_line, 0, zz).wait_recv()
            second(zz, 0).wait_recv()
            second(zz, 1).wait_recv()

        def line_total(k, half):
            zz = (z + k) % 4
            if half == 0:
                return acc[zz * 4 + own_line, 0] + ra[0, zz].astype(F32) + r2a[zz].astype(F32)
            return acc[zz * 4 + own_line, 1] + rb[0, zz].astype(F32) + r2b[zz].astype(F32)

        for k in (2, 1, 3):
            for half in range(2):
                r3send[k, half] = line_total(k, half).astype(BF)
            third(k).start()
        for k in (1, 3, 2):
            third(k).wait_recv()
        total = []
        for half in range(2):
            mine = line_total(0, half)
            for k in (1, 2, 3):
                mine = mine + r3[k, half].astype(F32)
            total.append(mine.astype(BF))
        summed = jnp.concatenate(total, axis=0)
        spots = lax.broadcasted_iota(jnp.int32, (n * capacity, LIVE), 1) == idxt_ref[...]
        spots = jnp.where(spots, 1.0, 0.0).astype(BF)
        wide = jnp.dot(spots, summed, preferred_element_type=F32).astype(BF)
        back_send[...] = wide.reshape(n, capacity, cols)
        for off in range(n):
            give(off).start()
        dk_ref[...] = jnp.zeros(dk_ref.shape, BF)
        dv_ref[...] = jnp.zeros(dv_ref.shape, BF)

    @pl.when(span == 0)
    def _():
        copy_to(pool_send, pool_got, p_send, p_recv, me, other).wait_recv()
        matrix = pool_got[...]
        for p in range(n):
            copy_to(back_send.at[p], back.at[p], b_send.at[p], b_recv.at[p], me, other).wait_recv()
            tokens = lax.dot_general(
                matrix, back[p].astype(F32), (((0,), (0,)), ((), ())),
                precision=lax.Precision.HIGHEST, preferred_element_type=F32,
            ).astype(BF)
            if p < n // 2:
                dk_ref[:, p * cols : (p + 1) * cols] = tokens
            else:
                q = p - n // 2
                dv_ref[:, q * cols : (q + 1) * cols] = tokens

    for off in range(1, n):
        spread(off).wait_send()
    for half in range(2):
        for k in range(1, 4):
            move(me, half, z_send.at[k, half], along_z(k)).wait_send()
    for k in range(4):
        block = along_z(k)
        for half in range(2):
            move(block, half, xy_send.at[k, 0, half], xn).wait_send()
            move(block, half, xy_send.at[k, 1, half], yn).wait_send()
        move(k * 4 + x_line, 0, f_send.at[k, 0], yn).wait_send()
        move(k * 4 + y_line, 1, f_send.at[k, 1], xn).wait_send()

    @pl.when(span == 1)
    def _():
        copy_to(pool_send, pool_got, p_send, p_recv, me, other).wait_send()
        for zz in range(4):
            send_b(x_line, 0, zz).wait_send()
            send_a(y_line, 0, zz).wait_send()
            send_a(d_line, 1, zz).wait_send()
            send_b(d_line, 1, zz).wait_send()
            second(zz, 0).wait_send()
            second(zz, 1).wait_send()
        for k in range(1, 4):
            third(k).wait_send()
        for off in range(n):
            give(off).wait_send()


def per_device_fused(query, dout, mem_key, mem_value, keep_count, keep_slot, pool_weight):
    n = 16
    tokens, width = query.shape[1:]
    capacity = mem_key.shape[1]
    cols = 2 * width // n
    counts = keep_count[0]
    ends = jnp.cumsum(counts)
    within = jnp.arange(capacity, dtype=jnp.int32)
    place = jnp.where(
        within[None, :] < counts[:, None], (ends - counts)[:, None] + within[None, :], -1
    ).reshape(1, n * capacity)
    vmem = pl.BlockSpec(memory_space=pltpu.VMEM)
    dma = pltpu.SemaphoreType.DMA
    out = jax.ShapeDtypeStruct((tokens, width), BF)
    half = (HALF, cols)
    dq, dk, dv = pl.pallas_call(
        fused_kernel,
        out_shape=(out, out, out),
        in_specs=[vmem] * 8,
        out_specs=(vmem, vmem, vmem),
        scratch_shapes=[
            pltpu.VMEM((n, capacity, cols), BF),
            pltpu.VMEM((n, capacity, cols), BF),
            pltpu.VMEM((n, 2) + half, BF),
            pltpu.VMEM((n, 2) + half, F32),
            pltpu.VMEM((n, 2) + half, BF),
            pltpu.VMEM((2, 4) + half, BF),
            pltpu.VMEM((2, 4) + half, BF),
            pltpu.VMEM((4,) + half, BF),
            pltpu.VMEM((4,) + half, BF),
            pltpu.VMEM((4, 2) + half, BF),
            pltpu.VMEM((4, 2) + half, BF),
            pltpu.VMEM((4, 2) + half, BF),
            pltpu.VMEM((n, capacity, cols), BF),
            pltpu.VMEM((n, capacity, cols), BF),
            pltpu.VMEM((capacity, tokens), F32),
            pltpu.VMEM((capacity, tokens), F32),
            dma((n,)), dma((n,)), dma((4, 2)), dma((4, 2, 2)), dma((4, 2)), dma((n, 2)),
            dma((2, 2, 4)), dma((2, 4)), dma((2, 4)), dma((4, 2)), dma((4, 2)), dma((4,)), dma((4,)),
            dma((n,)), dma((n,)), dma, dma,
        ],
        compiler_params=pltpu.CompilerParams(
            collective_id=0, has_side_effects=True, vmem_limit_bytes=48 << 20
        ),
    )(
        query[0], dout[0], mem_key[0], mem_value[0], place, place.reshape(n * capacity, 1),
        keep_slot[0], pool_weight[0],
    )
    return dq[None], dk[None], dv[None]


def solution(mesh):
    fused = mesh.shape["seq"] == 16 and mesh.shape["span"] == 2
    return jax.shard_map(
        per_device_fused if fused else per_device,
        mesh=mesh,
        in_specs=(
            P("span", "seq", None),
            P("span", "seq", None),
            P("span", "seq", None),
            P("span", "seq", None),
            P("span", None),
            P("span", "seq", None),
            P("span", "seq", None),
        ),
        out_specs=(P("span", "seq", None), P("span", "seq", None), P("span", "seq", None)),
        check_vma=False,
    )
```

```python
import math

import jax
import jax.numpy as jnp
from jax import lax
from jax.experimental import pallas as pl
from jax.experimental.pallas import tpu as pltpu
from jax.sharding import PartitionSpec as P

HEAD_DIM = 128
LIVE = 256
HALF = LIVE // 2
BF = jnp.bfloat16
F32 = jnp.float32
THIRD = F32
BACK = F32


def passed_along(block, axis, distance):
    devices = range(lax.axis_size(axis))
    route = [(i - distance, i) for i in devices if i - distance in devices]
    return lax.ppermute(block, axis, route)


def head_backward(query_head, grad_head, key_head, value_head, live_mask, block_rows):
    score_scale = key_head.shape[1] ** (-0.5)
    head_width = query_head.shape[1]
    blocks = query_head.shape[0] // block_rows
    query_blocks = query_head.reshape(blocks, block_rows, head_width)
    grad_blocks = grad_head.reshape(blocks, block_rows, head_width)

    def visit_block(totals, inputs):
        key_grad, value_grad = totals
        query_block, grad_block = inputs
        scores = jnp.dot(query_block, key_head.T, preferred_element_type=jnp.float32) * score_scale
        scores = jnp.where(live_mask[None, :], scores, -jnp.inf)
        shifted = jnp.exp(scores - jnp.max(scores, axis=1, keepdims=True))
        probs_full = shifted / jnp.sum(shifted, axis=1, keepdims=True)
        probs_low = probs_full.astype(jnp.bfloat16)
        attn_out = jnp.dot(probs_low, value_head, preferred_element_type=jnp.float32)
        deltas = jnp.sum(grad_block.astype(jnp.float32) * attn_out, axis=1, keepdims=True)
        probs_grad = jnp.dot(grad_block, value_head.T, preferred_element_type=jnp.float32)
        scores_grad = (probs_full * (probs_grad - deltas)).astype(jnp.bfloat16)
        query_grad = (
            jnp.dot(scores_grad, key_head, preferred_element_type=jnp.float32) * score_scale
        ).astype(jnp.bfloat16)
        key_grad = (
            key_grad
            + lax.dot_general(
                scores_grad,
                query_block,
                (((0,), (0,)), ((), ())),
                preferred_element_type=jnp.float32,
            )
            * score_scale
        )
        value_grad = value_grad + lax.dot_general(
            probs_low, grad_block, (((0,), (0,)), ((), ())), preferred_element_type=jnp.float32
        )
        return ((key_grad, value_grad), query_grad)

    empty_grad = jnp.zeros(key_head.shape, jnp.float32)
    (key_grad, value_grad), query_grad = lax.scan(
        visit_block, (empty_grad, empty_grad), (query_blocks, grad_blocks)
    )
    return (query_grad.reshape(-1, head_width), key_grad, value_grad)


def owner_rows(key_parts, value_parts, token_parts, groups, row_count):
    got_key, got_value = (
        lax.all_to_all(key_parts, "seq", split_axis=0, concat_axis=0, tiled=True),
        lax.all_to_all(value_parts, "seq", split_axis=0, concat_axis=0, tiled=True),
    )

    def fold_parts(values):
        shaped = values.reshape(token_parts, groups, row_count, values.shape[2], values.shape[3])
        summed = jnp.sum(shaped, axis=0)
        return summed.transpose(1, 0, 2, 3).reshape(row_count, -1)

    return (fold_parts(got_key), fold_parts(got_value))


def pool_matrix(slots, weights, local_tokens):
    positions = jnp.arange(local_tokens)
    onehot = (slots[:, :, None] == positions[None, None, :]).astype(jnp.float32)
    return jnp.einsum("cjt,cj->tc", onehot, weights, precision=lax.Precision.HIGHEST)


def apply_pool(matrix, key_rows, value_rows):
    stacked = jnp.concatenate([key_rows, value_rows], axis=1)
    return jnp.dot(
        matrix, stacked, precision=lax.Precision.HIGHEST, preferred_element_type=jnp.float32
    )


def per_device(query, dout, mem_key, mem_value, keep_count, keep_slot, pool_weight):
    devices = lax.axis_size("seq")
    head_width = HEAD_DIM
    head_count = query.shape[2] // head_width
    groups = math.gcd(head_count, devices)
    token_parts = devices // groups
    group_heads = head_count // groups
    local_tokens = query.shape[1]
    part_rows = local_tokens // token_parts
    capacity = mem_key.shape[1]
    owner_counts = keep_count[0]

    def token_layout(values):
        shaped = values.reshape(token_parts, part_rows, groups, group_heads, head_width)
        return shaped.transpose(0, 2, 1, 3, 4).reshape(devices, part_rows, group_heads, head_width)

    def memory_layout(values):
        row_count = values.shape[0]
        shaped = values.reshape(row_count, groups, group_heads, head_width).transpose(1, 0, 2, 3)
        spread = jnp.broadcast_to(shaped[None], (token_parts,) + shaped.shape)
        return spread.reshape(devices, row_count, group_heads, head_width)

    slot_index = jnp.arange(devices * capacity)
    live_mask = slot_index % capacity < jnp.repeat(owner_counts, capacity)
    key_used, value_used = (mem_key[0], mem_value[0])
    query_rows = lax.all_to_all(
        token_layout(query[0]), "seq", split_axis=0, concat_axis=0, tiled=True
    )
    grad_rows = lax.all_to_all(
        token_layout(dout[0]), "seq", split_axis=0, concat_axis=0, tiled=True
    )
    key_rows = lax.all_to_all(
        memory_layout(key_used), "seq", split_axis=0, concat_axis=0, tiled=True
    )
    value_rows = lax.all_to_all(
        memory_layout(value_used), "seq", split_axis=0, concat_axis=0, tiled=True
    )
    item_heads = query_rows.shape[2]
    row_count = key_rows.shape[1]
    query_total = devices * part_rows
    block_rows = 512
    query_flat = jnp.moveaxis(query_rows.reshape(query_total, item_heads, head_width), 1, 0)
    grad_flat = jnp.moveaxis(grad_rows.reshape(query_total, item_heads, head_width), 1, 0)
    key_flat = jnp.moveaxis(key_rows.reshape(devices * row_count, item_heads, head_width), 1, 0)
    value_flat = jnp.moveaxis(value_rows.reshape(devices * row_count, item_heads, head_width), 1, 0)

    def one_head(pieces):
        return head_backward(pieces[0], pieces[1], pieces[2], pieces[3], live_mask, block_rows)

    query_grad, key_grad, value_grad = lax.map(
        one_head, (query_flat, grad_flat, key_flat, value_flat)
    )
    query_back = jnp.moveaxis(query_grad, 0, 1).reshape(devices, part_rows, item_heads, head_width)
    key_back = jnp.moveaxis(key_grad, 0, 1).reshape(devices, row_count, item_heads, head_width)
    value_back = jnp.moveaxis(value_grad, 0, 1).reshape(devices, row_count, item_heads, head_width)
    returned = lax.all_to_all(query_back, "seq", split_axis=0, concat_axis=0, tiled=True)
    returned = returned.reshape(token_parts, groups, part_rows, group_heads, head_width).transpose(
        0, 2, 1, 3, 4
    )
    dquery = returned.reshape(1, local_tokens, groups * group_heads * head_width)
    matrix = pool_matrix(keep_slot[0], pool_weight[0], local_tokens)
    key_rows, value_rows = owner_rows(key_back, value_back, token_parts, groups, capacity)
    local_grad = apply_pool(matrix, key_rows, value_rows).astype(jnp.bfloat16)
    tokens_grad = passed_along(local_grad, "span", -1)
    feature_width = groups * group_heads * head_width
    dkey_tok = tokens_grad[None, :, :feature_width]
    dvalue_tok = tokens_grad[None, :, feature_width:]
    return (dquery, dkey_tok, dvalue_tok)


def copy_to(src, dst, send_sem, recv_sem, seq, span):
    return pltpu.make_async_remote_copy(
        src_ref=src,
        dst_ref=dst,
        send_sem=send_sem,
        recv_sem=recv_sem,
        device_id={"seq": seq, "span": span},
        device_id_type=pl.DeviceIdType.MESH,
    )


def fused_kernel(
    q_hbm, g_hbm, k_hbm, v_hbm, count_ref, slot_ref, weight_ref,
    dq_ref, dk_ref, dv_ref,
    q_ref, g_ref, k_ref, v_ref, picks_ref,
    kvin, rows, kv, acc, out16, ra, rb, r2a, r2b, r2send, r3, r3send, back_send, back,
    pool_send, pool_got,
    in_sem, a_send, a_recv, z_send, z_recv, xy_send, f_send, kv_recv,
    r1_send, ra_recv, rb_recv, r2_send, r2_recv, r3_send, r3_recv,
    b_send, b_recv, p_send, p_recv,
):
    n = 16
    parts = kv.shape[0]
    wide = HEAD_DIM
    me = lax.axis_index("seq")
    span = lax.axis_index("span")
    other = 1 - span
    capacity = k_ref.shape[0]
    z, y, x = me // 4, (me // 2) % 2, me % 2
    xn = me + 1 - 2 * x
    yn = me + 2 - 4 * y
    own_line = me % 4
    x_line = xn % 4
    y_line = yn % 4
    d_line = 3 - own_line
    scale = HEAD_DIM ** (-0.5)
    last = (((1,), (1,)), ((), ()))
    first = (((0,), (0,)), ((), ()))

    loads = [
        pltpu.make_async_copy(src, dst, in_sem.at[i])
        for i, (src, dst) in enumerate(((k_hbm, k_ref), (v_hbm, v_ref), (q_hbm, q_ref), (g_hbm, g_ref)))
    ]
    for load in loads:
        load.start()
    barrier = pltpu.get_barrier_semaphore()
    for off in range(1, n):
        pl.semaphore_signal(
            barrier, inc=1, device_id={"seq": (me + off) % n, "span": span},
            device_id_type=pl.DeviceIdType.MESH,
        )
    for off in range(n):
        pl.semaphore_signal(
            barrier, inc=1, device_id={"seq": (me + off) % n, "span": other},
            device_id_type=pl.DeviceIdType.MESH,
        )
    loads[0].wait()
    loads[1].wait()
    for part in range(parts):
        for p in range(n // 2):
            here = slice((p * parts + part) * wide, (p * parts + part + 1) * wide)
            kvin[part, p] = k_ref[:, here]
            kvin[part, n // 2 + p] = v_ref[:, here]
    pl.semaphore_wait(barrier, 2 * n - 1)

    def spread(part, off):
        p = (me + off) % n
        return copy_to(kvin.at[part, p], rows.at[part, me], a_send.at[part, off], a_recv.at[part, me], p, span)

    for part in range(parts):
        for off in range(1, n):
            spread(part, off).start()
        rows[part, me] = kvin[part, me]

    @pl.when(span == 1)
    def _():
        spots = lax.broadcasted_iota(jnp.int32, pool_send.shape, 0)
        total = jnp.zeros(pool_send.shape, F32)
        for j in range(slot_ref.shape[0]):
            total = total + jnp.where(spots == slot_ref[j : j + 1, :], weight_ref[j : j + 1, :], 0.0)
        pool_send[...] = total
        copy_to(pool_send, pool_got, p_send, p_recv, me, other).start()

    slots = n * capacity
    counts = jnp.broadcast_to(count_ref[...], (8, n)).astype(F32).astype(BF)
    owner = lax.broadcasted_iota(jnp.int32, (n, slots), 1)
    below = lax.broadcasted_iota(jnp.int32, (n, slots), 0) * capacity
    ahead = jnp.where(owner >= below + capacity, 1.0, 0.0).astype(BF)
    inside = jnp.where((owner >= below) & (owner < below + capacity), 1.0, 0.0).astype(BF)
    position = jnp.where((owner >= below) & (owner < below + capacity), owner - below, 0)
    position = jnp.sum(position.astype(F32), axis=0, keepdims=True)
    offset = jnp.dot(counts, ahead, preferred_element_type=F32)[:1]
    length = jnp.dot(counts, inside, preferred_element_type=F32)[:1]
    place = jnp.where(position < length, offset + position, -1.0).astype(jnp.int32)
    picks = lax.broadcasted_iota(jnp.int32, (LIVE, slots), 0) == place
    picks_ref[...] = jnp.where(picks, 1.0, 0.0).astype(BF)

    def along_z(k):
        return ((z + k) % 4) * 4 + own_line

    def column(part, k):
        mine = kv.at[part, own_line, :, z]
        return copy_to(mine, mine, z_send.at[part, k], z_recv.at[part, z], along_z(k), span)

    def column_in(part, k):
        block = kv.at[part, own_line, :, (z + k) % 4]
        return copy_to(block, block, z_send.at[part, k], z_recv.at[part, (z + k) % 4], along_z(k), span)

    def line_move(part, line, half, sem, target):
        block = kv.at[part, line, half]
        return copy_to(block, block, sem, kv_recv.at[part, line, half], target, span)

    def to_x(part, half):
        return line_move(part, own_line, half, xy_send.at[part, 0, half], xn)

    def to_y(part, half):
        return line_move(part, own_line, half, xy_send.at[part, 1, half], yn)

    def onward_y(part):
        return line_move(part, x_line, 0, f_send.at[part, 0], yn)

    def onward_x(part):
        return line_move(part, y_line, 1, f_send.at[part, 1], xn)

    def arrived(part, line, half):
        line_move(part, line, half, f_send.at[part, 0], xn).wait_recv()

    def pack(part):
        for off in range(1, n):
            p = (me + off) % n
            copy_to(kvin.at[part, p], rows.at[part, p], a_send.at[part, off], a_recv.at[part, p], p, span).wait_recv()
        packed = jnp.dot(picks_ref[...], rows[part].reshape(slots, wide), preferred_element_type=F32)
        kv[part, own_line, :, z] = packed.astype(BF).reshape(2, HALF, wide)
        for k in (2, 1, 3):
            column(part, k).start()

    def share(part):
        for k in (1, 3, 2):
            column_in(part, k).wait_recv()
        to_x(part, 0).start()
        to_y(part, 1).start()
        to_x(part, 1).start()
        to_y(part, 0).start()

    def forward(part):
        arrived(part, x_line, 0)
        onward_y(part).start()
        arrived(part, y_line, 1)
        onward_x(part).start()

    def send_a(part, line, slot):
        return copy_to(
            out16.at[part, line, 0], ra.at[part, slot], r1_send.at[part, 0, slot], ra_recv.at[part, slot], yn, span
        )

    def send_b(part, line, slot):
        return copy_to(
            out16.at[part, line, 1], rb.at[part, slot], r1_send.at[part, 1, slot], rb_recv.at[part, slot], xn, span
        )

    def compute_line(part, line):
        def triple(zz, carry):
            start = ((zz * 4 + line) * parts + part) * wide
            here = pl.ds(pl.multiple_of(start, 128), wide)
            query = q_ref[:, here]
            grad = g_ref[:, here]
            key = kv[part, line, :, zz].reshape(LIVE, wide)
            value = kv[part, line, :, zz + 2].reshape(LIVE, wide)
            scores = lax.dot_general(query, key, last, preferred_element_type=F32) * scale
            shifted = jnp.exp(scores - jnp.max(scores, axis=1, keepdims=True))
            probs = shifted / jnp.sum(shifted, axis=1, keepdims=True)
            low = probs.astype(BF)
            probs_grad = lax.dot_general(grad, value, last, preferred_element_type=F32)
            delta = jnp.sum(low.astype(F32) * probs_grad, axis=1, keepdims=True)
            scores_grad = (probs * (probs_grad - delta)).astype(BF)
            dq = jnp.dot(scores_grad, key, preferred_element_type=F32) * scale
            dq_ref[:, here] = dq.astype(BF)

            @pl.when(span == 1)
            def _():
                dkey = lax.dot_general(scores_grad, query, first, preferred_element_type=F32)
                dkey = (dkey * scale).reshape(2, HALF, wide)
                dvalue = lax.dot_general(low, grad, first, preferred_element_type=F32)
                dvalue = dvalue.reshape(2, HALF, wide)
                acc[part, line, :, zz] = dkey
                acc[part, line, :, zz + 2] = dvalue
                out16[part, line, :, zz] = dkey.astype(BF)
                out16[part, line, :, zz + 2] = dvalue.astype(BF)

            return carry

        lax.fori_loop(0, 2, triple, 0, unroll=True)

    def compute(part):
        compute_line(part, own_line)
        arrived(part, x_line, 1)
        compute_line(part, x_line)

        @pl.when(span == 1)
        def _():
            send_b(part, x_line, 0).start()

        arrived(part, y_line, 0)
        compute_line(part, y_line)

        @pl.when(span == 1)
        def _():
            send_a(part, y_line, 0).start()

        arrived(part, d_line, 0)
        arrived(part, d_line, 1)
        compute_line(part, d_line)

        @pl.when(span == 1)
        def _():
            send_a(part, d_line, 1).start()
            send_b(part, d_line, 1).start()

    def second_a(part):
        return copy_to(r2send.at[part, 0], r2a.at[part], r2_send.at[part, 0], r2_recv.at[part, 0], xn, span)

    def second_b(part):
        return copy_to(r2send.at[part, 1], r2b.at[part], r2_send.at[part, 1], r2_recv.at[part, 1], yn, span)

    def reduce_second(part):
        @pl.when(span == 1)
        def _():
            send_a(part, d_line, 1).wait_recv()
            r2send[part, 0] = (acc[part, x_line, 0] + ra[part, 1].astype(F32)).astype(BF)
            second_a(part).start()
            send_b(part, d_line, 1).wait_recv()
            r2send[part, 1] = (acc[part, y_line, 1] + rb[part, 1].astype(F32)).astype(BF)
            second_b(part).start()

    def third(part, k):
        return copy_to(
            r3send.at[part, k], r3.at[part, k], r3_send.at[part, k], r3_recv.at[part, k], along_z(k), span
        )

    def line_total(part, k):
        zz = (z + k) % 4
        upper = acc[part, own_line, 0, zz] + ra[part, 0, zz].astype(F32) + r2a[part, zz].astype(F32)
        lower = acc[part, own_line, 1, zz] + rb[part, 0, zz].astype(F32) + r2b[part, zz].astype(F32)
        return jnp.concatenate([upper, lower], axis=0)

    def reduce_third(part):
        @pl.when(span == 1)
        def _():
            send_a(part, y_line, 0).wait_recv()
            send_b(part, x_line, 0).wait_recv()
            second_a(part).wait_recv()
            second_b(part).wait_recv()
            for k in (2, 1, 3):
                r3send[part, k] = line_total(part, k).astype(r3send.dtype)
                third(part, k).start()

    def give(part, off):
        p = (me + off) % n
        return copy_to(back_send.at[part, p], back.at[part, me], b_send.at[part, off], b_recv.at[part, me], p, other)

    def hand_back(part):
        @pl.when(span == 1)
        def _():
            total = line_total(part, 0)
            for k in (1, 3, 2):
                third(part, k).wait_recv()
                total = total + r3[part, k].astype(F32)
            high = total.astype(BF)
            owned = lax.dot_general(picks_ref[...], high, first, preferred_element_type=F32)
            if back_send.dtype == F32:
                rest = (total - high.astype(F32)).astype(BF)
                owned = owned + lax.dot_general(picks_ref[...], rest, first, preferred_element_type=F32)
            back_send[part] = owned.astype(back_send.dtype).reshape(n, capacity, wide)
            for off in range(n):
                give(part, off).start()

    pack(0)
    pack(1)
    share(0)
    pack(2)
    share(1)
    forward(0)
    loads[2].wait()
    loads[3].wait()
    compute(0)
    share(2)
    forward(1)
    compute(1)
    reduce_second(0)
    forward(2)
    reduce_third(0)
    compute(2)
    reduce_second(1)
    hand_back(0)
    reduce_third(1)
    reduce_second(2)
    hand_back(1)
    reduce_third(2)
    hand_back(2)

    @pl.when(span == 1)
    def _():
        dk_ref[...] = jnp.zeros(dk_ref.shape, BF)
        dv_ref[...] = jnp.zeros(dv_ref.shape, BF)

    @pl.when(span == 0)
    def _():
        copy_to(pool_send, pool_got, p_send, p_recv, me, other).wait_recv()
        matrix = pool_got[...]
        for part in range(parts):
            for p in range(n):
                copy_to(
                    back_send.at[part, p], back.at[part, p], b_send.at[part, p], b_recv.at[part, p], me, other
                ).wait_recv()
            for p in range(n):
                tokens = jnp.dot(
                    matrix, back[part, p].astype(F32),
                    precision=lax.Precision.HIGHEST, preferred_element_type=F32,
                ).astype(BF)
                start = ((p % (n // 2)) * parts + part) * wide
                if p < n // 2:
                    dk_ref[:, start : start + wide] = tokens
                else:
                    dv_ref[:, start : start + wide] = tokens

    for part in range(parts):
        for off in range(1, n):
            spread(part, off).wait_send()
        for k in (1, 2, 3):
            column(part, k).wait_send()
        for half in range(2):
            to_x(part, half).wait_send()
            to_y(part, half).wait_send()
        onward_y(part).wait_send()
        onward_x(part).wait_send()

    @pl.when(span == 1)
    def _():
        copy_to(pool_send, pool_got, p_send, p_recv, me, other).wait_send()
        for part in range(parts):
            send_b(part, x_line, 0).wait_send()
            send_a(part, y_line, 0).wait_send()
            send_a(part, d_line, 1).wait_send()
            send_b(part, d_line, 1).wait_send()
            second_a(part).wait_send()
            second_b(part).wait_send()
            for k in (1, 2, 3):
                third(part, k).wait_send()
            for off in range(n):
                give(part, off).wait_send()


def per_device_fused(query, dout, mem_key, mem_value, keep_count, keep_slot, pool_weight):
    n = 16
    tokens, width = query.shape[1:]
    capacity = mem_key.shape[1]
    parts = 2 * width // n // HEAD_DIM
    vmem = pl.BlockSpec(memory_space=pltpu.VMEM)
    hbm = pl.BlockSpec(memory_space=pl.ANY)
    dma = pltpu.SemaphoreType.DMA
    out = jax.ShapeDtypeStruct((tokens, width), BF)
    half = (HALF, HEAD_DIM)
    owned = (parts, n, capacity, HEAD_DIM)
    dq, dk, dv = pl.pallas_call(
        fused_kernel,
        out_shape=(out, out, out),
        in_specs=[hbm] * 4 + [vmem] * 3,
        out_specs=(vmem, vmem, vmem),
        scratch_shapes=[
            pltpu.VMEM((tokens, width), BF),
            pltpu.VMEM((tokens, width), BF),
            pltpu.VMEM((capacity, width), BF),
            pltpu.VMEM((capacity, width), BF),
            pltpu.VMEM((LIVE, n * capacity), BF),
            pltpu.VMEM(owned, BF),
            pltpu.VMEM(owned, BF),
            pltpu.VMEM((parts, 4, 2, 4) + half, BF),
            pltpu.VMEM((parts, 4, 2, 4) + half, F32),
            pltpu.VMEM((parts, 4, 2, 4) + half, BF),
            pltpu.VMEM((parts, 2, 4) + half, BF),
            pltpu.VMEM((parts, 2, 4) + half, BF),
            pltpu.VMEM((parts, 4) + half, BF),
            pltpu.VMEM((parts, 4) + half, BF),
            pltpu.VMEM((parts, 2, 4) + half, BF),
            pltpu.VMEM((parts, 4, LIVE, HEAD_DIM), THIRD),
            pltpu.VMEM((parts, 4, LIVE, HEAD_DIM), THIRD),
            pltpu.VMEM(owned, BACK),
            pltpu.VMEM(owned, BACK),
            pltpu.VMEM((tokens, capacity), F32),
            pltpu.VMEM((tokens, capacity), F32),
            dma((4,)),
            dma((parts, n)), dma((parts, n)), dma((parts, 4)), dma((parts, 4)), dma((parts, 2, 2)),
            dma((parts, 2)), dma((parts, 4, 2)),
            dma((parts, 2, 2)), dma((parts, 2)), dma((parts, 2)), dma((parts, 2)), dma((parts, 2)),
            dma((parts, 4)), dma((parts, 4)),
            dma((parts, n)), dma((parts, n)), dma, dma,
        ],
        compiler_params=pltpu.CompilerParams(
            collective_id=0, has_side_effects=True, vmem_limit_bytes=56 << 20
        ),
    )(
        query[0], dout[0], mem_key[0], mem_value[0], keep_count, keep_slot[0].T, pool_weight[0].T,
    )
    return dq[None], dk[None], dv[None]


def solution(mesh):
    fused = mesh.shape["seq"] == 16 and mesh.shape["span"] == 2
    return jax.shard_map(
        per_device_fused if fused else per_device,
        mesh=mesh,
        in_specs=(
            P("span", "seq", None),
            P("span", "seq", None),
            P("span", "seq", None),
            P("span", "seq", None),
            P("span", None),
            P("span", "seq", None),
            P("span", "seq", None),
        ),
        out_specs=(P("span", "seq", None), P("span", "seq", None), P("span", "seq", None)),
        check_vma=False,
    )
```

```python
import math

import jax
import jax.numpy as jnp
from jax import lax
from jax.experimental import pallas as pl
from jax.experimental.pallas import tpu as pltpu
from jax.sharding import PartitionSpec as P

HEAD_DIM = 128
LIVE = 256
HALF = LIVE // 2
BF = jnp.bfloat16
F32 = jnp.float32
THIRD = F32
BACK = F32


def passed_along(block, axis, distance):
    devices = range(lax.axis_size(axis))
    route = [(i - distance, i) for i in devices if i - distance in devices]
    return lax.ppermute(block, axis, route)


def head_backward(query_head, grad_head, key_head, value_head, live_mask, block_rows):
    score_scale = key_head.shape[1] ** (-0.5)
    head_width = query_head.shape[1]
    blocks = query_head.shape[0] // block_rows
    query_blocks = query_head.reshape(blocks, block_rows, head_width)
    grad_blocks = grad_head.reshape(blocks, block_rows, head_width)

    def visit_block(totals, inputs):
        key_grad, value_grad = totals
        query_block, grad_block = inputs
        scores = jnp.dot(query_block, key_head.T, preferred_element_type=jnp.float32) * score_scale
        scores = jnp.where(live_mask[None, :], scores, -jnp.inf)
        shifted = jnp.exp(scores - jnp.max(scores, axis=1, keepdims=True))
        probs_full = shifted / jnp.sum(shifted, axis=1, keepdims=True)
        probs_low = probs_full.astype(jnp.bfloat16)
        attn_out = jnp.dot(probs_low, value_head, preferred_element_type=jnp.float32)
        deltas = jnp.sum(grad_block.astype(jnp.float32) * attn_out, axis=1, keepdims=True)
        probs_grad = jnp.dot(grad_block, value_head.T, preferred_element_type=jnp.float32)
        scores_grad = (probs_full * (probs_grad - deltas)).astype(jnp.bfloat16)
        query_grad = (
            jnp.dot(scores_grad, key_head, preferred_element_type=jnp.float32) * score_scale
        ).astype(jnp.bfloat16)
        key_grad = (
            key_grad
            + lax.dot_general(
                scores_grad,
                query_block,
                (((0,), (0,)), ((), ())),
                preferred_element_type=jnp.float32,
            )
            * score_scale
        )
        value_grad = value_grad + lax.dot_general(
            probs_low, grad_block, (((0,), (0,)), ((), ())), preferred_element_type=jnp.float32
        )
        return ((key_grad, value_grad), query_grad)

    empty_grad = jnp.zeros(key_head.shape, jnp.float32)
    (key_grad, value_grad), query_grad = lax.scan(
        visit_block, (empty_grad, empty_grad), (query_blocks, grad_blocks)
    )
    return (query_grad.reshape(-1, head_width), key_grad, value_grad)


def owner_rows(key_parts, value_parts, token_parts, groups, row_count):
    got_key, got_value = (
        lax.all_to_all(key_parts, "seq", split_axis=0, concat_axis=0, tiled=True),
        lax.all_to_all(value_parts, "seq", split_axis=0, concat_axis=0, tiled=True),
    )

    def fold_parts(values):
        shaped = values.reshape(token_parts, groups, row_count, values.shape[2], values.shape[3])
        summed = jnp.sum(shaped, axis=0)
        return summed.transpose(1, 0, 2, 3).reshape(row_count, -1)

    return (fold_parts(got_key), fold_parts(got_value))


def pool_matrix(slots, weights, local_tokens):
    positions = jnp.arange(local_tokens)
    onehot = (slots[:, :, None] == positions[None, None, :]).astype(jnp.float32)
    return jnp.einsum("cjt,cj->tc", onehot, weights, precision=lax.Precision.HIGHEST)


def apply_pool(matrix, key_rows, value_rows):
    stacked = jnp.concatenate([key_rows, value_rows], axis=1)
    return jnp.dot(
        matrix, stacked, precision=lax.Precision.HIGHEST, preferred_element_type=jnp.float32
    )


def per_device(query, dout, mem_key, mem_value, keep_count, keep_slot, pool_weight):
    devices = lax.axis_size("seq")
    head_width = HEAD_DIM
    head_count = query.shape[2] // head_width
    groups = math.gcd(head_count, devices)
    token_parts = devices // groups
    group_heads = head_count // groups
    local_tokens = query.shape[1]
    part_rows = local_tokens // token_parts
    capacity = mem_key.shape[1]
    owner_counts = keep_count[0]

    def token_layout(values):
        shaped = values.reshape(token_parts, part_rows, groups, group_heads, head_width)
        return shaped.transpose(0, 2, 1, 3, 4).reshape(devices, part_rows, group_heads, head_width)

    def memory_layout(values):
        row_count = values.shape[0]
        shaped = values.reshape(row_count, groups, group_heads, head_width).transpose(1, 0, 2, 3)
        spread = jnp.broadcast_to(shaped[None], (token_parts,) + shaped.shape)
        return spread.reshape(devices, row_count, group_heads, head_width)

    slot_index = jnp.arange(devices * capacity)
    live_mask = slot_index % capacity < jnp.repeat(owner_counts, capacity)
    key_used, value_used = (mem_key[0], mem_value[0])
    query_rows = lax.all_to_all(
        token_layout(query[0]), "seq", split_axis=0, concat_axis=0, tiled=True
    )
    grad_rows = lax.all_to_all(
        token_layout(dout[0]), "seq", split_axis=0, concat_axis=0, tiled=True
    )
    key_rows = lax.all_to_all(
        memory_layout(key_used), "seq", split_axis=0, concat_axis=0, tiled=True
    )
    value_rows = lax.all_to_all(
        memory_layout(value_used), "seq", split_axis=0, concat_axis=0, tiled=True
    )
    item_heads = query_rows.shape[2]
    row_count = key_rows.shape[1]
    query_total = devices * part_rows
    block_rows = 512
    query_flat = jnp.moveaxis(query_rows.reshape(query_total, item_heads, head_width), 1, 0)
    grad_flat = jnp.moveaxis(grad_rows.reshape(query_total, item_heads, head_width), 1, 0)
    key_flat = jnp.moveaxis(key_rows.reshape(devices * row_count, item_heads, head_width), 1, 0)
    value_flat = jnp.moveaxis(value_rows.reshape(devices * row_count, item_heads, head_width), 1, 0)

    def one_head(pieces):
        return head_backward(pieces[0], pieces[1], pieces[2], pieces[3], live_mask, block_rows)

    query_grad, key_grad, value_grad = lax.map(
        one_head, (query_flat, grad_flat, key_flat, value_flat)
    )
    query_back = jnp.moveaxis(query_grad, 0, 1).reshape(devices, part_rows, item_heads, head_width)
    key_back = jnp.moveaxis(key_grad, 0, 1).reshape(devices, row_count, item_heads, head_width)
    value_back = jnp.moveaxis(value_grad, 0, 1).reshape(devices, row_count, item_heads, head_width)
    returned = lax.all_to_all(query_back, "seq", split_axis=0, concat_axis=0, tiled=True)
    returned = returned.reshape(token_parts, groups, part_rows, group_heads, head_width).transpose(
        0, 2, 1, 3, 4
    )
    dquery = returned.reshape(1, local_tokens, groups * group_heads * head_width)
    matrix = pool_matrix(keep_slot[0], pool_weight[0], local_tokens)
    key_rows, value_rows = owner_rows(key_back, value_back, token_parts, groups, capacity)
    local_grad = apply_pool(matrix, key_rows, value_rows).astype(jnp.bfloat16)
    tokens_grad = passed_along(local_grad, "span", -1)
    feature_width = groups * group_heads * head_width
    dkey_tok = tokens_grad[None, :, :feature_width]
    dvalue_tok = tokens_grad[None, :, feature_width:]
    return (dquery, dkey_tok, dvalue_tok)


def copy_to(src, dst, send_sem, recv_sem, seq, span):
    return pltpu.make_async_remote_copy(
        src_ref=src,
        dst_ref=dst,
        send_sem=send_sem,
        recv_sem=recv_sem,
        device_id={"seq": seq, "span": span},
        device_id_type=pl.DeviceIdType.MESH,
    )


def fused_kernel(
    q_hbm, g_hbm, k_hbm, v_hbm, count_ref, slot_ref, weight_ref,
    dq_ref, dk_ref, dv_ref,
    q_ref, g_ref, k_ref, v_ref, picks_ref,
    kvin, rows, kv, acc, out16, ra, rb, r2a, r2b, r2send, r3, r3send, back_send, back,
    pool_send, pool_got,
    in_sem, a_send, a_recv, z_send, z_recv, xy_send, f_send, kv_recv,
    r1_send, ra_recv, rb_recv, r2_send, r2_recv, r3_send, r3_recv,
    b_send, b_recv, p_send, p_recv,
):
    n = 16
    parts = kv.shape[0]
    wide = HEAD_DIM
    me = lax.axis_index("seq")
    span = lax.axis_index("span")
    other = 1 - span
    capacity = k_ref.shape[0]
    z, y, x = me // 4, (me // 2) % 2, me % 2
    xn = me + 1 - 2 * x
    yn = me + 2 - 4 * y
    own_line = me % 4
    x_line = xn % 4
    y_line = yn % 4
    d_line = 3 - own_line
    scale = HEAD_DIM ** (-0.5)
    last = (((1,), (1,)), ((), ()))
    first = (((0,), (0,)), ((), ()))

    loads = [
        pltpu.make_async_copy(src, dst, in_sem.at[i])
        for i, (src, dst) in enumerate(((k_hbm, k_ref), (v_hbm, v_ref), (q_hbm, q_ref), (g_hbm, g_ref)))
    ]
    for load in loads:
        load.start()
    barrier = pltpu.get_barrier_semaphore()
    for off in range(1, n):
        pl.semaphore_signal(
            barrier, inc=1, device_id={"seq": (me + off) % n, "span": span},
            device_id_type=pl.DeviceIdType.MESH,
        )
    for off in range(n):
        pl.semaphore_signal(
            barrier, inc=1, device_id={"seq": (me + off) % n, "span": other},
            device_id_type=pl.DeviceIdType.MESH,
        )
    loads[0].wait()
    loads[1].wait()
    for part in range(parts):
        for p in range(n // 2):
            here = slice((p * parts + part) * wide, (p * parts + part + 1) * wide)
            kvin[part, p] = k_ref[:, here]
            kvin[part, n // 2 + p] = v_ref[:, here]
    pl.semaphore_wait(barrier, 2 * n - 1)

    def spread(part, off):
        p = (me + off) % n
        return copy_to(kvin.at[part, p], rows.at[part, me], a_send.at[part, off], a_recv.at[part, me], p, span)

    for part in range(parts):
        for off in range(1, n):
            spread(part, off).start()
        rows[part, me] = kvin[part, me]

    @pl.when(span == 1)
    def _():
        spots = lax.broadcasted_iota(jnp.int32, pool_send.shape, 0)
        total = jnp.zeros(pool_send.shape, F32)
        for j in range(slot_ref.shape[0]):
            total = total + jnp.where(spots == slot_ref[j : j + 1, :], weight_ref[j : j + 1, :], 0.0)
        pool_send[...] = total
        copy_to(pool_send, pool_got, p_send, p_recv, me, other).start()

    slots = n * capacity
    counts = jnp.broadcast_to(count_ref[...], (8, n)).astype(F32).astype(BF)
    owner = lax.broadcasted_iota(jnp.int32, (n, slots), 1)
    below = lax.broadcasted_iota(jnp.int32, (n, slots), 0) * capacity
    ahead = jnp.where(owner >= below + capacity, 1.0, 0.0).astype(BF)
    inside = jnp.where((owner >= below) & (owner < below + capacity), 1.0, 0.0).astype(BF)
    position = jnp.where((owner >= below) & (owner < below + capacity), owner - below, 0)
    position = jnp.sum(position.astype(F32), axis=0, keepdims=True)
    offset = jnp.dot(counts, ahead, preferred_element_type=F32)[:1]
    length = jnp.dot(counts, inside, preferred_element_type=F32)[:1]
    place = jnp.where(position < length, offset + position, -1.0).astype(jnp.int32)
    picks = lax.broadcasted_iota(jnp.int32, (LIVE, slots), 0) == place
    picks_ref[...] = jnp.where(picks, 1.0, 0.0).astype(BF)

    def along_z(k):
        return ((z + k) % 4) * 4 + own_line

    def column(part, k):
        mine = kv.at[part, own_line, :, z]
        return copy_to(mine, mine, z_send.at[part, k], z_recv.at[part, z], along_z(k), span)

    def column_in(part, k):
        block = kv.at[part, own_line, :, (z + k) % 4]
        return copy_to(block, block, z_send.at[part, k], z_recv.at[part, (z + k) % 4], along_z(k), span)

    def line_move(part, line, half, sem, target):
        block = kv.at[part, line, half]
        return copy_to(block, block, sem, kv_recv.at[part, line, half], target, span)

    def to_x(part, half):
        return line_move(part, own_line, half, xy_send.at[part, 0, half], xn)

    def to_y(part, half):
        return line_move(part, own_line, half, xy_send.at[part, 1, half], yn)

    def onward_y(part):
        return line_move(part, x_line, 0, f_send.at[part, 0], yn)

    def onward_x(part):
        return line_move(part, y_line, 1, f_send.at[part, 1], xn)

    def arrived(part, line, half):
        line_move(part, line, half, f_send.at[part, 0], xn).wait_recv()

    def pack(part):
        for off in range(1, n):
            p = (me + off) % n
            copy_to(kvin.at[part, p], rows.at[part, p], a_send.at[part, off], a_recv.at[part, p], p, span).wait_recv()
        packed = jnp.dot(picks_ref[...], rows[part].reshape(slots, wide), preferred_element_type=F32)
        kv[part, own_line, :, z] = packed.astype(BF).reshape(2, HALF, wide)
        for k in (2, 1, 3):
            column(part, k).start()

    def share(part):
        for k in (1, 3, 2):
            column_in(part, k).wait_recv()
        to_x(part, 0).start()
        to_y(part, 1).start()
        to_x(part, 1).start()
        to_y(part, 0).start()

    def forward(part):
        arrived(part, x_line, 0)
        onward_y(part).start()
        arrived(part, y_line, 1)
        onward_x(part).start()

    def send_a(part, line, slot):
        return copy_to(
            out16.at[part, line, 0], ra.at[part, slot], r1_send.at[part, 0, slot], ra_recv.at[part, slot], yn, span
        )

    def send_b(part, line, slot):
        return copy_to(
            out16.at[part, line, 1], rb.at[part, slot], r1_send.at[part, 1, slot], rb_recv.at[part, slot], xn, span
        )

    def compute_line(part, line):
        def triple(zz, carry):
            start = ((zz * 4 + line) * parts + part) * wide
            here = pl.ds(pl.multiple_of(start, 128), wide)
            query = q_ref[:, here]
            grad = g_ref[:, here]
            key = kv[part, line, :, zz].reshape(LIVE, wide)
            value = kv[part, line, :, zz + 2].reshape(LIVE, wide)
            scores = lax.dot_general(query, key, last, preferred_element_type=F32) * scale
            shifted = jnp.exp(scores - jnp.max(scores, axis=1, keepdims=True))
            probs = shifted / jnp.sum(shifted, axis=1, keepdims=True)
            low = probs.astype(BF)
            probs_grad = lax.dot_general(grad, value, last, preferred_element_type=F32)
            delta = jnp.sum(low.astype(F32) * probs_grad, axis=1, keepdims=True)
            scores_grad = (probs * (probs_grad - delta)).astype(BF)
            dq = jnp.dot(scores_grad, key, preferred_element_type=F32) * scale
            dq_ref[:, here] = dq.astype(BF)

            @pl.when(span == 1)
            def _():
                dkey = lax.dot_general(scores_grad, query, first, preferred_element_type=F32)
                dkey = (dkey * scale).reshape(2, HALF, wide)
                dvalue = lax.dot_general(low, grad, first, preferred_element_type=F32)
                dvalue = dvalue.reshape(2, HALF, wide)
                acc[part, line, :, zz] = dkey
                acc[part, line, :, zz + 2] = dvalue
                out16[part, line, :, zz] = dkey.astype(BF)
                out16[part, line, :, zz + 2] = dvalue.astype(BF)

            return carry

        lax.fori_loop(0, 2, triple, 0, unroll=True)

    def compute(part):
        compute_line(part, own_line)
        arrived(part, x_line, 1)
        compute_line(part, x_line)

        @pl.when(span == 1)
        def _():
            send_b(part, x_line, 0).start()

        arrived(part, y_line, 0)
        compute_line(part, y_line)

        @pl.when(span == 1)
        def _():
            send_a(part, y_line, 0).start()

        arrived(part, d_line, 0)
        arrived(part, d_line, 1)
        compute_line(part, d_line)

        @pl.when(span == 1)
        def _():
            send_a(part, d_line, 1).start()
            send_b(part, d_line, 1).start()

    def second_a(part):
        return copy_to(r2send.at[part, 0], r2a.at[part], r2_send.at[part, 0], r2_recv.at[part, 0], xn, span)

    def second_b(part):
        return copy_to(r2send.at[part, 1], r2b.at[part], r2_send.at[part, 1], r2_recv.at[part, 1], yn, span)

    def reduce_second(part):
        @pl.when(span == 1)
        def _():
            send_a(part, d_line, 1).wait_recv()
            r2send[part, 0] = (acc[part, x_line, 0] + ra[part, 1].astype(F32)).astype(BF)
            second_a(part).start()
            send_b(part, d_line, 1).wait_recv()
            r2send[part, 1] = (acc[part, y_line, 1] + rb[part, 1].astype(F32)).astype(BF)
            second_b(part).start()

    def third(part, k):
        return copy_to(
            r3send.at[part, k], r3.at[part, k], r3_send.at[part, k], r3_recv.at[part, k], along_z(k), span
        )

    def line_total(part, k):
        zz = (z + k) % 4
        upper = acc[part, own_line, 0, zz] + ra[part, 0, zz].astype(F32) + r2a[part, zz].astype(F32)
        lower = acc[part, own_line, 1, zz] + rb[part, 0, zz].astype(F32) + r2b[part, zz].astype(F32)
        return jnp.concatenate([upper, lower], axis=0)

    def reduce_third(part):
        @pl.when(span == 1)
        def _():
            send_a(part, y_line, 0).wait_recv()
            send_b(part, x_line, 0).wait_recv()
            second_a(part).wait_recv()
            second_b(part).wait_recv()
            for k in (2, 1, 3):
                r3send[part, k] = line_total(part, k).astype(r3send.dtype)
                third(part, k).start()

    def give(part, off):
        p = (me + off) % n
        return copy_to(back_send.at[part, p], back.at[part, me], b_send.at[part, off], b_recv.at[part, me], p, other)

    def hand_back(part):
        @pl.when(span == 1)
        def _():
            total = line_total(part, 0)
            for k in (1, 3, 2):
                third(part, k).wait_recv()
                total = total + r3[part, k].astype(F32)
            high = total.astype(BF)
            owned = lax.dot_general(picks_ref[...], high, first, preferred_element_type=F32)
            if back_send.dtype == F32:
                rest = (total - high.astype(F32)).astype(BF)
                owned = owned + lax.dot_general(picks_ref[...], rest, first, preferred_element_type=F32)
            back_send[part] = owned.astype(back_send.dtype).reshape(n, capacity, wide)
            for off in range(n):
                give(part, off).start()

    pack(0)
    share(0)
    pack(1)
    forward(0)
    share(1)
    pack(2)
    forward(1)
    share(2)
    loads[2].wait()
    loads[3].wait()
    compute(0)
    forward(2)
    compute(1)
    reduce_second(0)
    reduce_second(1)
    reduce_third(0)
    compute(2)
    reduce_third(1)
    hand_back(0)
    reduce_second(2)
    hand_back(1)
    reduce_third(2)
    hand_back(2)

    @pl.when(span == 1)
    def _():
        dk_ref[...] = jnp.zeros(dk_ref.shape, BF)
        dv_ref[...] = jnp.zeros(dv_ref.shape, BF)

    @pl.when(span == 0)
    def _():
        copy_to(pool_send, pool_got, p_send, p_recv, me, other).wait_recv()
        matrix = pool_got[...]
        for part in range(parts):
            for p in range(n):
                copy_to(
                    back_send.at[part, p], back.at[part, p], b_send.at[part, p], b_recv.at[part, p], me, other
                ).wait_recv()
            for p in range(n):
                tokens = jnp.dot(
                    matrix, back[part, p].astype(F32),
                    precision=lax.Precision.HIGHEST, preferred_element_type=F32,
                ).astype(BF)
                start = ((p % (n // 2)) * parts + part) * wide
                if p < n // 2:
                    dk_ref[:, start : start + wide] = tokens
                else:
                    dv_ref[:, start : start + wide] = tokens

    for part in range(parts):
        for off in range(1, n):
            spread(part, off).wait_send()
        for k in (1, 2, 3):
            column(part, k).wait_send()
        for half in range(2):
            to_x(part, half).wait_send()
            to_y(part, half).wait_send()
        onward_y(part).wait_send()
        onward_x(part).wait_send()

    @pl.when(span == 1)
    def _():
        copy_to(pool_send, pool_got, p_send, p_recv, me, other).wait_send()
        for part in range(parts):
            send_b(part, x_line, 0).wait_send()
            send_a(part, y_line, 0).wait_send()
            send_a(part, d_line, 1).wait_send()
            send_b(part, d_line, 1).wait_send()
            second_a(part).wait_send()
            second_b(part).wait_send()
            for k in (1, 2, 3):
                third(part, k).wait_send()
            for off in range(n):
                give(part, off).wait_send()


def per_device_fused(query, dout, mem_key, mem_value, keep_count, keep_slot, pool_weight):
    n = 16
    tokens, width = query.shape[1:]
    capacity = mem_key.shape[1]
    parts = 2 * width // n // HEAD_DIM
    vmem = pl.BlockSpec(memory_space=pltpu.VMEM)
    hbm = pl.BlockSpec(memory_space=pl.ANY)
    dma = pltpu.SemaphoreType.DMA
    out = jax.ShapeDtypeStruct((tokens, width), BF)
    half = (HALF, HEAD_DIM)
    owned = (parts, n, capacity, HEAD_DIM)
    dq, dk, dv = pl.pallas_call(
        fused_kernel,
        out_shape=(out, out, out),
        in_specs=[hbm] * 4 + [vmem] * 3,
        out_specs=(vmem, vmem, vmem),
        scratch_shapes=[
            pltpu.VMEM((tokens, width), BF),
            pltpu.VMEM((tokens, width), BF),
            pltpu.VMEM((capacity, width), BF),
            pltpu.VMEM((capacity, width), BF),
            pltpu.VMEM((LIVE, n * capacity), BF),
            pltpu.VMEM(owned, BF),
            pltpu.VMEM(owned, BF),
            pltpu.VMEM((parts, 4, 2, 4) + half, BF),
            pltpu.VMEM((parts, 4, 2, 4) + half, F32),
            pltpu.VMEM((parts, 4, 2, 4) + half, BF),
            pltpu.VMEM((parts, 2, 4) + half, BF),
            pltpu.VMEM((parts, 2, 4) + half, BF),
            pltpu.VMEM((parts, 4) + half, BF),
            pltpu.VMEM((parts, 4) + half, BF),
            pltpu.VMEM((parts, 2, 4) + half, BF),
            pltpu.VMEM((parts, 4, LIVE, HEAD_DIM), THIRD),
            pltpu.VMEM((parts, 4, LIVE, HEAD_DIM), THIRD),
            pltpu.VMEM(owned, BACK),
            pltpu.VMEM(owned, BACK),
            pltpu.VMEM((tokens, capacity), F32),
            pltpu.VMEM((tokens, capacity), F32),
            dma((4,)),
            dma((parts, n)), dma((parts, n)), dma((parts, 4)), dma((parts, 4)), dma((parts, 2, 2)),
            dma((parts, 2)), dma((parts, 4, 2)),
            dma((parts, 2, 2)), dma((parts, 2)), dma((parts, 2)), dma((parts, 2)), dma((parts, 2)),
            dma((parts, 4)), dma((parts, 4)),
            dma((parts, n)), dma((parts, n)), dma, dma,
        ],
        compiler_params=pltpu.CompilerParams(
            collective_id=0, has_side_effects=True, vmem_limit_bytes=56 << 20
        ),
    )(
        query[0], dout[0], mem_key[0], mem_value[0], keep_count, keep_slot[0].T, pool_weight[0].T,
    )
    return dq[None], dk[None], dv[None]


def solution(mesh):
    fused = mesh.shape["seq"] == 16 and mesh.shape["span"] == 2
    return jax.shard_map(
        per_device_fused if fused else per_device,
        mesh=mesh,
        in_specs=(
            P("span", "seq", None),
            P("span", "seq", None),
            P("span", "seq", None),
            P("span", "seq", None),
            P("span", None),
            P("span", "seq", None),
            P("span", "seq", None),
        ),
        out_specs=(P("span", "seq", None), P("span", "seq", None), P("span", "seq", None)),
        check_vma=False,
    )
```
